256 devices in a mesh: rows: 32 (over z_lo, y, core), rank: 8 (over z_hi, x).
Axes of the slice: x: 4, y: 4, z: 8 (z_hi: 2, z_lo: 4; z = z_hi * 4 + z_lo), core: 2. Of those that a mesh axis runs over, the one named last changes fastest.
Arguments:
- factor: bfloat16 [32768, 16384], P('rows', 'rank'), may hold values from -0.03125 to 0.03125
- probes: bfloat16 [32768, 256], P('rows'), may hold values from -1.5 to 1.5
- cotangent: bfloat16 [32768, 256], P('rows'), may hold values from -1.5 to 1.5
- core_inverse: bfloat16 [16384, 8, 2048], P('rank', None, 'rows'), may hold values from -0.046875 to 0.046875
- pivots: int32 [16384], replicated, may hold values from 0 to 32767, as said below
- noise: float32 [1], replicated, may hold values from 0.5 to 2
Outputs:
- probe_grad: bfloat16 [32768, 256], P('rows')
- factor_grad: bfloat16 [32768, 16384], P('rows', 'rank')
The draws below stay inside these ranges and needn't reach their ends.
Inputs may be any that keep to these rules, and one draw needn't show every extreme that they name: `pivots`: distinct slab rows; rows 0 and 32767 are always among them.
All inputs are finite; a program needn't handle non-finite values.
Results may differ from the reference program's by a relative error of at most 0.001.
Values sent between devices are 32-bit elements; how exact they have to be, the bound alone decides.
No kernel may reach another device: no remote copies, remote signals or barrier semaphores. Data moves between devices by JAX's collectives and lax.ppermute only.
A program may use at most 64 MiB of HBM per device.

```python
import math
import jax
import jax.numpy as jnp
from jax import lax

K = 16384
B = 256
NS = 32768
KB = 2048
N_RANK = 8


def draw_pivots(key, part):
    first = jax.random.fold_in(key, 11)
    second = jax.random.fold_in(key, 23)
    scores = jax.random.permutation(first, NS).astype(jnp.int32)
    scores = scores.at[0].set(-2).at[NS - 1].set(-1)
    order = jnp.argsort(scores, stable=True).astype(jnp.int32)
    chosen = order[:K]
    return jax.random.permutation(second, chosen).astype(jnp.int32)


def level_of(rng, dims, pieces, smallest, top_value):
    def one(axis_at, blocks):
        steps = jax.random.uniform(jax.random.fold_in(jax.random.fold_in(rng, 6), axis_at), (blocks,), jnp.float32, smallest / len(pieces), top_value / len(pieces))
        return jnp.repeat(jnp.exp(steps), dims[axis_at] // blocks).reshape((-1,) + (1,) * (len(dims) - axis_at - 1))

    loudness = one(*pieces[0])
    for cut in pieces[1:]:
        loudness = loudness * one(*cut)
    return loudness


def gaussian(key, shape, spread, bound, pieces=(), held_as=jnp.bfloat16):
    level = level_of(key, shape, pieces, -0.22, 0.18) if pieces else 1.0
    result = jax.random.normal(key, shape, jnp.float32) * spread * level
    return jnp.minimum(jnp.maximum(result, -bound), bound).astype(held_as)


def setup_inputs(seed: int = 0) -> dict:
    streams_of = jax.random.split(jax.random.key(seed), 7)
    factor = gaussian(streams_of[0], (NS, K), NS ** -0.5, 0.03125, ((0, 32), (1, 8)))
    probes = gaussian(streams_of[1], (NS, B), 0.25, 1.5, ((0, 32),))
    cotangent = gaussian(streams_of[2], (NS, B), 0.25, 1.5, ((0, 32),))
    core_inverse = gaussian(streams_of[3], (K, N_RANK, KB), K ** -0.5, 0.046875, ((0, 8), (2, 32)))
    pivots = draw_pivots(jax.random.fold_in(streams_of[6], 71), 0)
    noise = jnp.clip(jnp.exp(jax.random.uniform(streams_of[5], (1,), jnp.float32, math.log(0.5), math.log(2.0))), 0.5, 2.0)
    return dict(factor=factor, probes=probes, cotangent=cotangent, core_inverse=core_inverse, pivots=pivots, noise=noise)


def reference(factor, probes, cotangent, core_inverse, pivots, noise):
    scale = noise[0]
    highest = lax.Precision.HIGHEST
    contract = (((0,), (0,)), ((), ()))
    coefs = lax.dot_general(factor, probes, contract, preferred_element_type=jnp.float32)
    duals_in = lax.dot_general(factor, cotangent, contract, preferred_element_type=jnp.float32)
    kblock = min(K, 1024)
    core_blocks = core_inverse.reshape(K // kblock, kblock, K)

    def weight_block(core_blk):
        return jnp.dot(core_blk.astype(jnp.float32), coefs, precision=highest, preferred_element_type=jnp.float32)

    weights = lax.map(weight_block, core_blocks).reshape(K, B)

    def dual_step(carry, items):
        core_blk, dual_blk = items
        term = lax.dot_general(core_blk.astype(jnp.float32), dual_blk, contract, precision=highest, preferred_element_type=jnp.float32)
        return carry + term, None

    duals, unused = lax.scan(dual_step, jnp.zeros((K, B), jnp.float32), (core_blocks, duals_in.reshape(K // kblock, kblock, B)))
    pivot_rank = jnp.full((NS,), K, jnp.int32).at[pivots].set(jnp.arange(K, dtype=jnp.int32))
    block = min(NS, 1024)
    columns = jnp.arange(K, dtype=jnp.int32)

    def one_block(items):
        fac_blk, cot_blk, probe_blk, rank_blk = items
        correction = jnp.dot(fac_blk.astype(jnp.float32), duals, precision=highest, preferred_element_type=jnp.float32)
        pgrad = ((cot_blk.astype(jnp.float32) - correction) / scale).astype(jnp.bfloat16)
        first = lax.dot_general(cot_blk.astype(jnp.float32), weights, (((1,), (1,)), ((), ())), precision=highest, preferred_element_type=jnp.float32)
        second = lax.dot_general(probe_blk.astype(jnp.float32), duals, (((1,), (1,)), ((), ())), precision=highest, preferred_element_type=jnp.float32)
        grads = -(first + second) / scale
        grads = jnp.where(columns[None, :] > rank_blk[:, None], jnp.float32(0.0), grads)
        return pgrad, grads.astype(jnp.bfloat16)

    probe_grad, factor_grad = lax.map(one_block, (factor.reshape(NS // block, block, K), cotangent.reshape(NS // block, block, B), probes.reshape(NS // block, block, B), pivot_rank.reshape(NS // block, block)))
    return probe_grad.reshape(NS, B), factor_grad.reshape(NS, K)
```

```python
import jax
import jax.numpy as jnp
from jax import lax
from jax.experimental import pallas as pl
from jax.experimental.pallas import tpu as pltpu
from jax.sharding import PartitionSpec as P


PARTS = {
    "z": ("rows", 4, 8),
    "y": ("rows", 4, 2),
    "core": ("rows", 2, 1),
    "zhi": ("rank", 2, 4),
    "x": ("rank", 4, 1),
}


def place_of(part):
    axis, members, stride = PARTS[part]
    return lax.rem(lax.axis_index(axis) // stride, members)


def shifted(value, part, step):
    axis, members, stride = PARTS[part]
    pairs = []
    for source in range(lax.axis_size(axis)):
        at = source // stride % members
        pairs.append((source, source + ((at + step) % members - at) * stride))
    return lax.ppermute(value, axis, pairs)


def pick(value, index, dim):
    return lax.dynamic_index_in_dim(value, index, dim, keepdims=False)


def scatter_sum(value, part, dim):
    members = PARTS[part][1]
    me = place_of(part)
    arrived = [
        shifted(pick(value, lax.rem(me + step, members), dim), part, step)
        for step in range(1, members)
    ]
    total = pick(value, me, dim)
    for piece in arrived:
        total = total + piece
    return total


def gather(value, part, dim):
    members = PARTS[part][1]
    me = place_of(part)
    shape = value.shape[:dim] + (members,) + value.shape[dim:]
    whole = jnp.zeros(shape, value.dtype)
    whole = lax.dynamic_update_index_in_dim(whole, value, me, dim)
    for step in range(1, members):
        piece = shifted(value, part, step)
        whole = lax.dynamic_update_index_in_dim(
            whole, piece, lax.rem(me - step + members, members), dim
        )
    return whole


def two_terms(value):
    head = lax.reduce_precision(value, 8, 7)
    return head.astype(jnp.bfloat16), (value - head).astype(jnp.bfloat16)


def wide_dot(exact, value, dims, split):
    head, rest = two_terms(value)
    both = jnp.concatenate((head, rest), axis=split)
    out = lax.dot_general(exact, both, (dims, ((), ())), preferred_element_type=jnp.float32)
    half = out.shape[1] // 2
    return out[:, :half] + out[:, half:]


def after(value, *others):
    return lax.optimization_barrier((value, *others))[0]


def ranks_of_rows(pivots, rows_dev):
    total = pivots.shape[0]
    fine = 32
    local = pivots - lax.axis_index("rows") * rows_dev
    coarse = lax.broadcasted_iota(jnp.int32, (rows_dev // fine, total), 0)
    in_coarse = ((local // fine)[None, :] == coarse) & (local >= 0)[None, :]
    at_fine = lax.rem(local, fine)[None, :] == lax.broadcasted_iota(jnp.int32, (fine, total), 0)
    column = lax.broadcasted_iota(jnp.int32, (fine, total), 1)
    values = jnp.concatenate(
        [jnp.where(at_fine, v, 0) for v in (jnp.ones_like(column), column // 128, column % 128)],
        axis=0,
    ).astype(jnp.bfloat16)
    found = lax.dot_general(
        in_coarse.astype(jnp.bfloat16),
        values,
        (((1,), (1,)), ((), ())),
        preferred_element_type=jnp.float32,
    )
    count, high, low = found[:, :fine], found[:, fine : 2 * fine], found[:, 2 * fine :]
    rank = jnp.where(count > 0.5, high * 128.0 + low, float(total)).astype(jnp.int32)
    return rank.reshape(rows_dev)


def split_in_kernel(value):
    head = value.astype(jnp.bfloat16)
    return head, (value - head.astype(jnp.float32)).astype(jnp.bfloat16)


LAST_LAST = (((1,), (1,)), ((), ()))
LAST_FIRST = (((1,), (0,)), ((), ()))


def dot32(left, right, dims):
    return lax.dot_general(left, right, dims, preferred_element_type=jnp.float32)


def correction_kernel(factor_ref, duals_ref, out_ref, head_ref, rest_ref):
    @pl.when(pl.program_id(0) == 0)
    def _():
        head_ref[...], rest_ref[...] = split_in_kernel(duals_ref[...])

    block = factor_ref[...]
    out_ref[...] = dot32(block, head_ref[...], LAST_FIRST) + dot32(block, rest_ref[...], LAST_FIRST)


def factor_times(factor, duals):
    rows, cols = factor.shape
    width = duals.shape[1]
    tile = 256
    return pl.pallas_call(
        correction_kernel,
        grid=(rows // tile,),
        in_specs=[
            pl.BlockSpec((tile, cols), lambda i: (i, 0)),
            pl.BlockSpec((cols, width), lambda i: (0, 0), pipeline_mode=pl.Buffered(1)),
        ],
        out_specs=pl.BlockSpec((tile, width), lambda i: (i, 0)),
        out_shape=jax.ShapeDtypeStruct((rows, width), jnp.float32),
        scratch_shapes=[pltpu.VMEM((cols, width), jnp.bfloat16)] * 2,
        cost_estimate=pl.CostEstimate(
            flops=4 * rows * cols * width,
            transcendentals=0,
            bytes_accessed=2 * rows * cols + 4 * cols * width + 4 * rows * width,
        ),
        name="factor_times",
    )(factor, duals)


def outer_kernel(scale_ref, first_ref, cot_ref, probe_ref, weights_ref, duals_ref, rank_ref, out_ref):
    w_head, w_rest = split_in_kernel(weights_ref[...])
    d_head, d_rest = split_in_kernel(duals_ref[...])
    cot, probe = cot_ref[...], probe_ref[...]
    total = dot32(cot, w_head, LAST_FIRST) + dot32(cot, w_rest, LAST_FIRST)
    total = total + dot32(probe, d_head, LAST_LAST) + dot32(probe, d_rest, LAST_LAST)
    column = lax.broadcasted_iota(jnp.int32, total.shape, 1)
    column = column + (first_ref[0] + pl.program_id(0) * total.shape[1])
    total = total * (-1.0 / scale_ref[0])
    out_ref[...] = jnp.where(column > rank_ref[...], 0.0, total).astype(jnp.bfloat16)


def masked_outer(scale, first, cotangent, probes, weights, duals, pivot_rank):
    rows, width = cotangent.shape
    cols = duals.shape[0]
    tile = 256
    whole = pl.BlockSpec((rows, width), lambda j: (0, 0), pipeline_mode=pl.Buffered(1))
    return pl.pallas_call(
        outer_kernel,
        grid=(cols // tile,),
        in_specs=[
            pl.BlockSpec(memory_space=pltpu.SMEM),
            pl.BlockSpec(memory_space=pltpu.SMEM),
            whole,
            whole,
            pl.BlockSpec((width, tile), lambda j: (0, j)),
            pl.BlockSpec((tile, width), lambda j: (j, 0)),
            pl.BlockSpec((rows, 1), lambda j: (0, 0), pipeline_mode=pl.Buffered(1)),
        ],
        out_specs=pl.BlockSpec((rows, tile), lambda j: (0, j)),
        out_shape=jax.ShapeDtypeStruct((rows, cols), jnp.bfloat16),
        cost_estimate=pl.CostEstimate(
            flops=8 * rows * cols * width,
            transcendentals=0,
            bytes_accessed=2 * rows * cols + 8 * cols * width + 4 * rows * width,
        ),
        name="masked_outer",
    )(scale, first, cotangent, probes, weights, duals, pivot_rank)


def body(factor, probes, cotangent, core_inverse, pivots, noise):
    rows_dev, block_cols = factor.shape
    width = probes.shape[1]
    n_rows = lax.axis_size("rows")
    n_rank = lax.axis_size("rank")
    slim = block_cols // n_rows
    scale = noise[0]
    core_tile = core_inverse.reshape(block_cols, n_rank * slim)
    contract = ((0,), (0,))

    dual = lax.dot_general(cotangent, factor, (contract, ((), ())), preferred_element_type=jnp.float32)
    coef = lax.dot_general(
        after(factor, dual), probes, (contract, ((), ())), preferred_element_type=jnp.float32
    )

    dual = scatter_sum(dual.reshape(2, width // 2, block_cols), "core", 0)
    coef = after(coef.reshape(4, 4, 2, slim, width), dual)
    coef = scatter_sum(coef, "core", 2)
    dual = scatter_sum(dual.reshape(4, width // 8, block_cols), "y", 0)
    coef = scatter_sum(after(coef, dual), "y", 1)
    dual = scatter_sum(dual.reshape(4, width // 32, block_cols), "z", 0)
    dual = gather(dual, "z", 0).reshape(width // 8, block_cols)
    coef = scatter_sum(after(coef, dual), "z", 0)
    dual = gather(dual, "y", 0).reshape(width // 2, block_cols)
    dual = gather(dual, "core", 0).reshape(width, block_cols)
    coef = gather(coef, "zhi", 0)

    duals = wide_dot(core_tile, dual, ((0,), (1,)), 0)
    coef = gather(after(coef, duals), "x", 1).reshape(n_rank * slim, width)
    duals = scatter_sum(duals.reshape(2, 4, slim, width), "x", 1)

    head, rest = two_terms(coef)
    weights = lax.dot_general(head, core_tile, ((((0,), (1,))), ((), ())), preferred_element_type=jnp.float32)
    weights = weights + lax.dot_general(
        rest, core_tile, ((((0,), (1,))), ((), ())), preferred_element_type=jnp.float32
    )
    weights = after(weights, duals)
    duals = scatter_sum(duals, "zhi", 0)
    weights = scatter_sum(weights.reshape(2, width // 2, block_cols), "core", 0)
    weights = after(weights, duals)
    duals = gather(duals, "z", 0)
    weights = scatter_sum(weights.reshape(4, width // 8, block_cols), "y", 0)
    weights = after(weights, duals)
    duals = gather(duals, "y", 1)
    weights = scatter_sum(weights.reshape(4, width // 32, block_cols), "z", 0)
    duals = gather(duals, "core", 2).reshape(block_cols, width)
    weights = gather(after(weights, duals), "z", 0).reshape(width // 8, block_cols)

    correction = factor_times(factor, duals)
    correction = scatter_sum(correction.reshape(4, rows_dev // 4, width), "x", 0)
    weights = gather(after(weights, correction), "y", 0).reshape(width // 2, block_cols)
    correction = correction + shifted(correction, "zhi", 1)
    weights = gather(after(weights, correction), "core", 0).reshape(width, block_cols)
    correction = gather(correction, "x", 0).reshape(rows_dev, width)
    probe_grad = ((cotangent.astype(jnp.float32) - correction) / scale).astype(jnp.bfloat16)

    pivot_rank = ranks_of_rows(pivots, rows_dev)
    first = (lax.axis_index("rank") * block_cols).astype(jnp.int32).reshape(1)
    grads = masked_outer(noise, first, cotangent, probes, weights, duals, pivot_rank.reshape(rows_dev, 1))
    return (probe_grad, grads)


def solution(mesh):
    placed = (
        P("rows", "rank"),
        P("rows", None),
        P("rows", None),
        P("rank", None, "rows"),
        P(),
        P(),
    )
    return jax.shard_map(
        body,
        mesh=mesh,
        in_specs=placed,
        out_specs=(P("rows", None), P("rows", "rank")),
        check_vma=False,
    )
```

```python
import jax
import jax.numpy as jnp
from jax import lax
from jax.experimental import pallas as pl
from jax.experimental.pallas import tpu as pltpu
from jax.sharding import PartitionSpec as P


PARTS = {
    "z": ("rows", 4, 8),
    "y": ("rows", 4, 2),
    "core": ("rows", 2, 1),
    "zhi": ("rank", 2, 4),
    "x": ("rank", 4, 1),
}


def place_of(part):
    axis, members, stride = PARTS[part]
    return lax.rem(lax.axis_index(axis) // stride, members)


def sent(value, part, move):
    axis, members, stride = PARTS[part]
    pairs = []
    for source in range(lax.axis_size(axis)):
        at = source // stride % members
        pairs.append((source, source + (move(at) - at) * stride))
    return lax.ppermute(value, axis, pairs)


def shifted(value, part, step):
    members = PARTS[part][1]
    return sent(value, part, lambda at: (at + step) % members)


def swapped(value, part, mask):
    return sent(value, part, lambda at: at ^ mask)


def pick(value, index, dim):
    return lax.dynamic_index_in_dim(value, index, dim, keepdims=False)


def put(whole, value, index, dim):
    return lax.dynamic_update_index_in_dim(whole, value, index, dim)


def scatter_sum(value, part, dim):
    members = PARTS[part][1]
    me = place_of(part)
    arrived = [
        shifted(pick(value, lax.rem(me + step, members), dim), part, step)
        for step in range(1, members)
    ]
    total = pick(value, me, dim)
    for piece in arrived:
        total = total + piece
    return total


def gather(value, part, dim):
    members = PARTS[part][1]
    me = place_of(part)
    shape = value.shape[:dim] + (members,) + value.shape[dim:]
    whole = put(jnp.zeros(shape, value.dtype), value, me, dim)
    for step in range(1, members):
        piece = shifted(value, part, step)
        whole = put(whole, piece, lax.rem(me - step + members, members), dim)
    return whole


def pair_sum(value, part, dim):
    me = place_of(part)
    return pick(value, me, dim) + swapped(pick(value, 1 - me, dim), part, 1)


def pair_gather(value, part, dim):
    me = place_of(part)
    whole = put(jnp.zeros(value.shape[:dim] + (2,) + value.shape[dim:], value.dtype), value, me, dim)
    return put(whole, swapped(value, part, 1), 1 - me, dim)


def passed_on(value):
    return sent(value, "y", lambda at: (at + 3) % 4)


def halves_sum(low, high, part, first, second):
    return low + swapped(low, part, first), high + swapped(high, part, second)


def two_terms(value):
    head = lax.reduce_precision(value, 8, 7)
    return head.astype(jnp.bfloat16), (value - head).astype(jnp.bfloat16)


def wide_dot(exact, value, dims, split):
    head, rest = two_terms(value)
    both = jnp.concatenate((head, rest), axis=split)
    out = lax.dot_general(exact, both, (dims, ((), ())), preferred_element_type=jnp.float32)
    half = out.shape[1] // 2
    return out[:, :half] + out[:, half:]


def after(value, *others):
    return lax.optimization_barrier((value, *others))[0]


def together(*values):
    return lax.optimization_barrier(values)


def ranks_of_rows(pivots, rows_dev):
    total = pivots.shape[0]
    fine = 32
    local = pivots - lax.axis_index("rows") * rows_dev
    coarse = lax.broadcasted_iota(jnp.int32, (rows_dev // fine, total), 0)
    in_coarse = ((local // fine)[None, :] == coarse) & (local >= 0)[None, :]
    at_fine = lax.rem(local, fine)[None, :] == lax.broadcasted_iota(jnp.int32, (fine, total), 0)
    column = lax.broadcasted_iota(jnp.int32, (fine, total), 1)
    values = jnp.concatenate(
        [jnp.where(at_fine, v, 0) for v in (jnp.ones_like(column), column // 128, column % 128)],
        axis=0,
    ).astype(jnp.bfloat16)
    found = lax.dot_general(
        in_coarse.astype(jnp.bfloat16),
        values,
        (((1,), (1,)), ((), ())),
        preferred_element_type=jnp.float32,
    )
    count, high, low = found[:, :fine], found[:, fine : 2 * fine], found[:, 2 * fine :]
    rank = jnp.where(count > 0.5, high * 128.0 + low, float(total)).astype(jnp.int32)
    return rank.reshape(rows_dev)


def split_in_kernel(value):
    head = value.astype(jnp.bfloat16)
    return head, (value - head.astype(jnp.float32)).astype(jnp.bfloat16)


LAST_FIRST = (((1,), (0,)), ((), ()))


def dot32(left, right, dims):
    return lax.dot_general(left, right, dims, preferred_element_type=jnp.float32)


def correction_kernel(factor_ref, duals_ref, out_ref, head_ref, rest_ref):
    @pl.when(pl.program_id(0) == 0)
    def _():
        head_ref[...], rest_ref[...] = split_in_kernel(duals_ref[...])

    block = factor_ref[...]
    out_ref[...] = dot32(block, head_ref[...], LAST_FIRST) + dot32(block, rest_ref[...], LAST_FIRST)


def factor_times(factor, duals):
    rows, cols = factor.shape
    width = duals.shape[1]
    tile = min(256, rows)
    return pl.pallas_call(
        correction_kernel,
        grid=(rows // tile,),
        in_specs=[
            pl.BlockSpec((tile, cols), lambda i: (i, 0)),
            pl.BlockSpec((cols, width), lambda i: (0, 0), pipeline_mode=pl.Buffered(1)),
        ],
        out_specs=pl.BlockSpec((tile, width), lambda i: (i, 0)),
        out_shape=jax.ShapeDtypeStruct((rows, width), jnp.float32),
        scratch_shapes=[pltpu.VMEM((cols, width), jnp.bfloat16)] * 2,
        cost_estimate=pl.CostEstimate(
            flops=4 * rows * cols * width,
            transcendentals=0,
            bytes_accessed=2 * rows * cols + 4 * cols * width + 4 * rows * width,
        ),
        name="factor_times",
    )(factor, duals)


def outer_kernel(
    scale_ref, first_ref, cot_ref, probe_ref, weights_ref, duals_ref, rank_ref, out_ref, left_ref
):
    @pl.when(pl.program_id(0) == 0)
    def _():
        left_ref[...] = jnp.concatenate([cot_ref[...], cot_ref[...], probe_ref[...], probe_ref[...]], axis=1)

    right = jnp.concatenate(
        split_in_kernel(weights_ref[...]) + split_in_kernel(duals_ref[...].T), axis=0
    )
    total = dot32(left_ref[...], right, LAST_FIRST) * (-1.0 / scale_ref[0])
    column = lax.broadcasted_iota(jnp.int32, total.shape, 1)
    limit = rank_ref[...] - (first_ref[0] + pl.program_id(0) * total.shape[1])
    out_ref[...] = jnp.where(column > limit, 0.0, total).astype(jnp.bfloat16)


def masked_outer(scale, first, cotangent, probes, weights, duals, pivot_rank):
    rows, width = cotangent.shape
    cols = duals.shape[0]
    tile = 256
    whole = pl.BlockSpec((rows, width), lambda j: (0, 0), pipeline_mode=pl.Buffered(1))
    return pl.pallas_call(
        outer_kernel,
        grid=(cols // tile,),
        in_specs=[
            pl.BlockSpec(memory_space=pltpu.SMEM),
            pl.BlockSpec(memory_space=pltpu.SMEM),
            whole,
            whole,
            pl.BlockSpec((width, tile), lambda j: (0, j)),
            pl.BlockSpec((tile, width), lambda j: (j, 0)),
            pl.BlockSpec((rows, 1), lambda j: (0, 0), pipeline_mode=pl.Buffered(1)),
        ],
        out_specs=pl.BlockSpec((rows, tile), lambda j: (0, j)),
        out_shape=jax.ShapeDtypeStruct((rows, cols), jnp.bfloat16),
        scratch_shapes=[pltpu.VMEM((rows, 4 * width), jnp.bfloat16)],
        cost_estimate=pl.CostEstimate(
            flops=8 * rows * cols * width,
            transcendentals=0,
            bytes_accessed=2 * rows * cols + 8 * cols * width + 4 * rows * width,
        ),
        name="masked_outer",
    )(scale, first, cotangent, probes, weights, duals, pivot_rank)


def body(factor, probes, cotangent, core_inverse, pivots, noise):
    rows_dev, block_cols = factor.shape
    width = probes.shape[1]
    n_rows = lax.axis_size("rows")
    n_rank = lax.axis_size("rank")
    slim = block_cols // n_rows
    scale = noise[0]
    core_tile = core_inverse.reshape(block_cols, n_rank * slim)
    contract = ((0,), (0,))

    dual = lax.dot_general(cotangent, factor, (contract, ((), ())), preferred_element_type=jnp.float32)
    coef = lax.dot_general(
        after(factor, dual), probes, (contract, ((), ())), preferred_element_type=jnp.float32
    )

    dual = pair_sum(dual.reshape(2, width // 2, block_cols), "core", 0)

    coef = pair_sum(after(coef.reshape(4, 4, 2, slim, width), dual), "core", 2)
    dual = scatter_sum(dual.reshape(4, width // 8, block_cols), "y", 0)

    dual, coef = together(dual, coef)
    coef = scatter_sum(coef, "y", 1)
    low, high = halves_sum(dual[: width // 16], dual[width // 16 :], "z", 1, 2)
    low, high = halves_sum(low, high, "z", 2, 1)
    dual = jnp.concatenate([low, high], axis=0)

    dual, coef = together(dual, coef)
    coef = scatter_sum(coef, "z", 0)
    dual = gather(dual, "y", 0).reshape(width // 2, block_cols)

    dual, coef = together(dual, coef)
    coef = pair_gather(coef, "zhi", 0)
    dual = pair_gather(dual, "core", 0).reshape(width, block_cols)

    duals = wide_dot(core_tile, dual, ((0,), (1,)), 0)
    coef = after(coef, duals)
    duals = scatter_sum(duals.reshape(2, 4, slim, width), "x", 1)
    me_x = place_of("x")
    near = jnp.stack([coef, swapped(coef, "x", 3)])
    duals, near = together(duals, near)
    far = swapped(near, "x", 1)
    duals = pair_sum(duals, "zhi", 0)
    whole = jnp.zeros((2, 4, slim, width), jnp.float32)
    for piece, mask in ((near[0], 0), (near[1], 3), (far[0], 1), (far[1], 2)):
        whole = put(whole, piece, me_x ^ mask, 1)
    coef = whole.reshape(n_rank * slim, width)
    duals, coef = together(duals, coef)

    head, rest = two_terms(coef)
    weights = lax.dot_general(head, core_tile, (((0,), (1,)), ((), ())), preferred_element_type=jnp.float32)
    weights = weights + lax.dot_general(
        rest, core_tile, (((0,), (1,)), ((), ())), preferred_element_type=jnp.float32
    )
    weights = pair_sum(weights.reshape(2, width // 2, block_cols), "core", 0)
    duals = gather(duals, "z", 0)
    duals, weights = together(duals, weights)

    weights = weights.reshape(4, width // 8, block_cols)
    me_y = place_of("y")
    ring = passed_on(pick(weights, (me_y + 1) % 4, 0))
    ring = ring + pick(weights, (me_y + 2) % 4, 0)
    duals = gather(duals, "y", 1)
    ring = passed_on(ring)
    duals = pair_gather(duals, "core", 2).reshape(block_cols, width)
    ring = passed_on(ring + pick(weights, (me_y + 3) % 4, 0))
    weights = ring + pick(weights, me_y, 0)

    correction = factor_times(factor, duals)
    correction, weights = together(correction, weights)
    low, high = halves_sum(weights[: width // 16], weights[width // 16 :], "z", 1, 2)
    correction = scatter_sum(correction.reshape(4, rows_dev // 4, width), "x", 0)
    correction, low, high = together(correction, low, high)
    low, high = halves_sum(low, high, "z", 2, 1)
    correction = correction + swapped(correction, "zhi", 1)
    weights = jnp.concatenate([low, high], axis=0)

    weights = gather(weights, "y", 0).reshape(width // 2, block_cols)
    weights = pair_gather(weights, "core", 0).reshape(width, block_cols)
    correction = gather(correction, "x", 0).reshape(rows_dev, width)
    probe_grad = ((cotangent.astype(jnp.float32) - correction) / scale).astype(jnp.bfloat16)

    pivot_rank = ranks_of_rows(pivots, rows_dev)
    first = (lax.axis_index("rank") * block_cols).astype(jnp.int32).reshape(1)
    grads = masked_outer(noise, first, cotangent, probes, weights, duals, pivot_rank.reshape(rows_dev, 1))
    return (probe_grad, grads)


def solution(mesh):
    placed = (
        P("rows", "rank"),
        P("rows", None),
        P("rows", None),
        P("rank", None, "rows"),
        P(),
        P(),
    )
    return jax.shard_map(
        body,
        mesh=mesh,
        in_specs=placed,
        out_specs=(P("rows", None), P("rows", "rank")),
        check_vma=False,
    )
```

```python
import functools

import jax
import jax.numpy as jnp
from jax import lax
from jax.experimental import pallas as pl
from jax.experimental.pallas import tpu as pltpu
from jax.sharding import PartitionSpec as P


PARTS = {
    "z": ("rows", 4, 8),
    "y": ("rows", 4, 2),
    "core": ("rows", 2, 1),
    "zhi": ("rank", 2, 4),
    "x": ("rank", 4, 1),
}


def place_of(part):
    axis, members, stride = PARTS[part]
    return lax.rem(lax.axis_index(axis) // stride, members)


def sent(value, part, move):
    axis, members, stride = PARTS[part]
    pairs = []
    for source in range(lax.axis_size(axis)):
        at = source // stride % members
        pairs.append((source, source + (move(at) - at) * stride))
    return lax.ppermute(value, axis, pairs)


def shifted(value, part, step):
    members = PARTS[part][1]
    return sent(value, part, lambda at: (at + step) % members)


def swapped(value, part, mask):
    return sent(value, part, lambda at: at ^ mask)


def pick(value, index, dim):
    return lax.dynamic_index_in_dim(value, index, dim, keepdims=False)


def put(whole, value, index, dim):
    return lax.dynamic_update_index_in_dim(whole, value, index, dim)


def scatter_sum(value, part, dim):
    members = PARTS[part][1]
    me = place_of(part)
    arrived = [shifted(pick(value, lax.rem(me + step, members), dim), part, step) for step in range(1, members)]
    total = pick(value, me, dim)
    for piece in arrived:
        total = total + piece
    return total


def gather(value, part, dim):
    members = PARTS[part][1]
    me = place_of(part)
    shape = value.shape[:dim] + (members,) + value.shape[dim:]
    whole = put(jnp.zeros(shape, value.dtype), value, me, dim)
    for step in range(1, members):
        piece = shifted(value, part, step)
        whole = put(whole, piece, lax.rem(me - step + members, members), dim)
    return whole


def pair_sum(value, part, dim):
    me = place_of(part)
    return pick(value, me, dim) + swapped(pick(value, 1 - me, dim), part, 1)


def pair_gather(value, part, dim):
    me = place_of(part)
    whole = put(jnp.zeros(value.shape[:dim] + (2,) + value.shape[dim:], value.dtype), value, me, dim)
    return put(whole, swapped(value, part, 1), 1 - me, dim)


def halving(value, part, dim, first, second, ahead=()):
    me = place_of(part)
    away = jnp.stack([pick(value, me ^ first, dim), pick(value, me ^ first ^ second, dim)])
    got = swapped(away, part, first)
    other = pick(value, me ^ second, dim) + got[1]
    other = lax.optimization_barrier((other, *ahead))[0]
    return pick(value, me, dim) + got[0] + swapped(other, part, second)


def two_terms(value):
    head = lax.reduce_precision(value, 8, 7)
    return head.astype(jnp.bfloat16), (value - head).astype(jnp.bfloat16)


def wide_dot(exact, value, dims, split):
    head, rest = two_terms(value)
    both = jnp.concatenate((head, rest), axis=split)
    out = lax.dot_general(exact, both, (dims, ((), ())), preferred_element_type=jnp.float32)
    half = out.shape[1] // 2
    return out[:, :half] + out[:, half:]


def ranks_of_rows(pivots, rows_dev):
    total = pivots.shape[0]
    fine = 32
    local = pivots - lax.axis_index("rows") * rows_dev
    coarse = lax.broadcasted_iota(jnp.int32, (rows_dev // fine, total), 0)
    in_coarse = ((local // fine)[None, :] == coarse) & (local >= 0)[None, :]
    at_fine = lax.rem(local, fine)[None, :] == lax.broadcasted_iota(jnp.int32, (fine, total), 0)
    column = lax.broadcasted_iota(jnp.int32, (fine, total), 1)
    values = jnp.concatenate(
        [jnp.where(at_fine, v, 0) for v in (jnp.ones_like(column), column // 128, column % 128)],
        axis=0,
    ).astype(jnp.bfloat16)
    found = lax.dot_general(
        in_coarse.astype(jnp.bfloat16),
        values,
        (((1,), (1,)), ((), ())),
        preferred_element_type=jnp.float32,
    )
    count, high, low = found[:, :fine], found[:, fine : 2 * fine], found[:, 2 * fine :]
    rank = jnp.where(count > 0.5, high * 128.0 + low, float(total)).astype(jnp.int32)
    return rank.reshape(rows_dev)


def split_in_kernel(value):
    head = value.astype(jnp.bfloat16)
    return head, (value - head.astype(jnp.float32)).astype(jnp.bfloat16)


LAST_FIRST = (((1,), (0,)), ((), ()))


def dot32(left, right, dims):
    return lax.dot_general(left, right, dims, preferred_element_type=jnp.float32)


def correction_kernel(core_ref, factor_ref, own_ref, other_ref, out_ref, head_ref, rest_ref, *, slim):
    @pl.when(pl.program_id(0) == 0)
    def _():
        for ref, place in ((own_ref, core_ref[0]), (other_ref, 1 - core_ref[0])):
            for block in range(ref.shape[0] // slim):
                rows = pl.ds(pl.multiple_of((2 * block + place) * slim, slim), slim)
                head_ref[rows, :], rest_ref[rows, :] = split_in_kernel(ref[pl.ds(block * slim, slim), :])

    block = factor_ref[...]
    out_ref[...] = dot32(block, head_ref[...], LAST_FIRST) + dot32(block, rest_ref[...], LAST_FIRST)


def factor_times(core, factor, own, other, slim):
    rows, cols = factor.shape
    width = own.shape[1]
    tile = min(256, rows)
    half = pl.BlockSpec((cols // 2, width), lambda i: (0, 0), pipeline_mode=pl.Buffered(1))
    return pl.pallas_call(
        functools.partial(correction_kernel, slim=slim),
        grid=(rows // tile,),
        in_specs=[
            pl.BlockSpec(memory_space=pltpu.SMEM),
            pl.BlockSpec((tile, cols), lambda i: (i, 0)),
            half,
            half,
        ],
        out_specs=pl.BlockSpec((tile, width), lambda i: (i, 0)),
        out_shape=jax.ShapeDtypeStruct((rows, width), jnp.float32),
        scratch_shapes=[pltpu.VMEM((cols, width), jnp.bfloat16)] * 2,
        cost_estimate=pl.CostEstimate(
            flops=4 * rows * cols * width,
            transcendentals=0,
            bytes_accessed=2 * rows * cols + 4 * cols * width + 4 * rows * width,
        ),
        name="factor_times",
    )(core, factor, own, other)


def outer_kernel(
    scale_ref, place_ref, cot_ref, probe_ref, w_own_ref, w_other_ref, d_own_ref, d_other_ref, rank_ref,
    out_ref, left_ref, *, slim,
):
    first_core = place_ref[1] == 0

    @pl.when(pl.program_id(0) == 0)
    def _():
        cot, probe = cot_ref[...], probe_ref[...]
        half = cot.shape[1] // 2
        turned = jnp.concatenate([cot[:, half:], cot[:, :half]], axis=1)
        cot = jnp.where(first_core, cot, turned)
        left_ref[...] = jnp.concatenate([cot, cot, probe, probe], axis=1)

    own, other = d_own_ref[...], d_other_ref[...]
    even, odd = jnp.where(first_core, own, other), jnp.where(first_core, other, own)
    blocks = []
    for at in range(0, own.shape[0], slim):
        blocks += [even[at : at + slim], odd[at : at + slim]]
    d_head, d_rest = split_in_kernel(jnp.concatenate(blocks, axis=0).T)
    own_head, own_rest = split_in_kernel(w_own_ref[...])
    other_head, other_rest = split_in_kernel(w_other_ref[...])
    right = jnp.concatenate([own_head, other_head, own_rest, other_rest, d_head, d_rest], axis=0)
    total = dot32(left_ref[...], right, LAST_FIRST) * (-1.0 / scale_ref[0])
    column = lax.broadcasted_iota(jnp.int32, total.shape, 1)
    limit = rank_ref[...] - (place_ref[0] + pl.program_id(0) * total.shape[1])
    out_ref[...] = jnp.where(column > limit, 0.0, total).astype(jnp.bfloat16)


def masked_outer(scale, place, cotangent, probes, w_own, w_other, d_own, d_other, pivot_rank, slim):
    rows, width = cotangent.shape
    cols = w_own.shape[1]
    tile = 256
    whole = pl.BlockSpec((rows, width), lambda j: (0, 0), pipeline_mode=pl.Buffered(1))
    w_spec = pl.BlockSpec((width // 2, tile), lambda j: (0, j))
    d_spec = pl.BlockSpec((tile // 2, width), lambda j: (j, 0))
    return pl.pallas_call(
        functools.partial(outer_kernel, slim=slim),
        grid=(cols // tile,),
        in_specs=[
            pl.BlockSpec(memory_space=pltpu.SMEM),
            pl.BlockSpec(memory_space=pltpu.SMEM),
            whole,
            whole,
            w_spec,
            w_spec,
            d_spec,
            d_spec,
            pl.BlockSpec((rows, 1), lambda j: (0, 0), pipeline_mode=pl.Buffered(1)),
        ],
        out_specs=pl.BlockSpec((rows, tile), lambda j: (0, j)),
        out_shape=jax.ShapeDtypeStruct((rows, cols), jnp.bfloat16),
        scratch_shapes=[pltpu.VMEM((rows, 4 * width), jnp.bfloat16)],
        cost_estimate=pl.CostEstimate(
            flops=8 * rows * cols * width,
            transcendentals=0,
            bytes_accessed=2 * rows * cols + 8 * cols * width + 4 * rows * width,
        ),
        name="masked_outer",
    )(scale, place, cotangent, probes, w_own, w_other, d_own, d_other, pivot_rank)


def body(factor, probes, cotangent, core_inverse, pivots, noise):
    rows_dev, block_cols = factor.shape
    width = probes.shape[1]
    n_rows = lax.axis_size("rows")
    n_rank = lax.axis_size("rank")
    slim = block_cols // n_rows
    scale = noise[0]
    core_tile = core_inverse.reshape(block_cols, n_rank * slim)
    contract = ((0,), (0,))

    dual = lax.dot_general(cotangent, factor, (contract, ((), ())), preferred_element_type=jnp.float32)
    coef = lax.dot_general(factor, probes, (contract, ((), ())), preferred_element_type=jnp.float32)
    pivot_rank = ranks_of_rows(pivots, rows_dev).reshape(rows_dev, 1)
    core = place_of("core").astype(jnp.int32).reshape(1)

    dual = pair_sum(dual.reshape(2, width // 2, block_cols), "core", 0)
    dual = halving(dual.reshape(4, width // 8, block_cols), "y", 0, 1, 3, (pivot_rank,))
    dual = dual + swapped(dual, "z", 2)
    dual = dual + swapped(dual, "z", 1)
    coef = pair_sum(coef.reshape(4, 4, 2, slim, width), "core", 2)
    coef = halving(coef, "y", 1, 3, 1)
    coef = halving(coef, "z", 0, 1, 2)

    dual = gather(dual, "y", 0).reshape(width // 2, block_cols)
    dual = pair_gather(dual, "core", 0).reshape(width, block_cols)
    coef = jnp.broadcast_to(coef[None], (n_rank, slim, width))
    coef = lax.all_to_all(coef, "rank", 0, 0).reshape(n_rank * slim, width)

    head, rest = two_terms(coef)
    weights = lax.dot_general(head, core_tile, (((0,), (1,)), ((), ())), preferred_element_type=jnp.float32)
    weights = weights + lax.dot_general(
        rest, core_tile, (((0,), (1,)), ((), ())), preferred_element_type=jnp.float32
    )
    duals = wide_dot(core_tile, dual, ((0,), (1,)), 0).reshape(n_rank, slim, width)
    duals = jnp.sum(lax.all_to_all(duals, "rank", 0, 0), axis=0)
    weights = pair_sum(weights.reshape(2, width // 2, block_cols), "core", 0)
    weights = halving(weights.reshape(4, width // 8, block_cols), "y", 0, 1, 3)

    duals = gather(duals, "z", 0)
    duals = gather(duals, "y", 1).reshape(block_cols // 2, width)
    duals_other = swapped(duals, "core", 1)
    correction = factor_times(core, factor, duals, duals_other, slim)
    weights = weights + swapped(weights, "z", 2)
    arrived = lax.optimization_barrier((swapped(weights, "z", 1), correction))[0]
    weights = gather(weights + arrived, "y", 0).reshape(width // 2, block_cols)
    weights_other = swapped(weights, "core", 1)

    correction = scatter_sum(correction.reshape(4, rows_dev // 4, width), "x", 0)
    correction = correction + swapped(correction, "zhi", 1)
    correction = gather(correction, "x", 0).reshape(rows_dev, width)
    probe_grad = ((cotangent.astype(jnp.float32) - correction) / scale).astype(jnp.bfloat16)

    first = (lax.axis_index("rank") * block_cols).astype(jnp.int32).reshape(1)
    grads = masked_outer(
        noise, jnp.concatenate([first, core]), cotangent, probes,
        weights, weights_other, duals, duals_other, pivot_rank, slim,
    )
    return (probe_grad, grads)


def solution(mesh):
    placed = (
        P("rows", "rank"),
        P("rows", None),
        P("rows", None),
        P("rank", None, "rows"),
        P(),
        P(),
    )
    return jax.shard_map(
        body,
        mesh=mesh,
        in_specs=placed,
        out_specs=(P("rows", None), P("rows", "rank")),
        check_vma=False,
    )
```

```python
import functools

import jax
import jax.numpy as jnp
from jax import lax
from jax.experimental import pallas as pl
from jax.experimental.pallas import tpu as pltpu
from jax.sharding import PartitionSpec as P


PARTS = {
    "z": ("rows", 4, 8),
    "y": ("rows", 4, 2),
    "core": ("rows", 2, 1),
    "zhi": ("rank", 2, 4),
    "x": ("rank", 4, 1),
}


def place_of(part):
    axis, members, stride = PARTS[part]
    return lax.rem(lax.axis_index(axis) // stride, members)


def sent(value, part, move):
    axis, members, stride = PARTS[part]
    pairs = []
    for source in range(lax.axis_size(axis)):
        at = source // stride % members
        pairs.append((source, source + (move(at) - at) * stride))
    return lax.ppermute(value, axis, pairs)


def shifted(value, part, step):
    members = PARTS[part][1]
    return sent(value, part, lambda at: (at + step) % members)


def swapped(value, part, mask):
    return sent(value, part, lambda at: at ^ mask)


def pick(value, index, dim):
    return lax.dynamic_index_in_dim(value, index, dim, keepdims=False)


def put(whole, value, index, dim):
    return lax.dynamic_update_index_in_dim(whole, value, index, dim)


def gather(value, part, dim):
    members = PARTS[part][1]
    me = place_of(part)
    value = lax.optimization_barrier(value)
    shape = value.shape[:dim] + (members,) + value.shape[dim:]
    whole = put(jnp.zeros(shape, value.dtype), value, me, dim)
    for step in range(1, members):
        piece = shifted(value, part, step)
        whole = put(whole, piece, lax.rem(me - step + members, members), dim)
    return whole


def pair_sum(value, part, dim):
    me = place_of(part)
    return pick(value, me, dim) + swapped(pick(value, 1 - me, dim), part, 1)


def halving(value, part, dim, first, second, ahead=()):
    me = place_of(part)
    away = jnp.stack([pick(value, me ^ first, dim), pick(value, me ^ first ^ second, dim)])
    got = swapped(away, part, first)
    other = pick(value, me ^ second, dim) + got[1]
    other = lax.optimization_barrier((other, *ahead))[0]
    return pick(value, me, dim) + got[0] + swapped(other, part, second)


def two_terms(value):
    head = lax.reduce_precision(value, 8, 7)
    return head.astype(jnp.bfloat16), (value - head).astype(jnp.bfloat16)


def ranks_of_rows(pivots, rows_dev):
    total = pivots.shape[0]
    fine = 32
    local = pivots - lax.axis_index("rows") * rows_dev
    coarse = lax.broadcasted_iota(jnp.int32, (rows_dev // fine, total), 0)
    in_coarse = ((local // fine)[None, :] == coarse) & (local >= 0)[None, :]
    at_fine = lax.rem(local, fine)[None, :] == lax.broadcasted_iota(jnp.int32, (fine, total), 0)
    column = lax.broadcasted_iota(jnp.int32, (fine, total), 1)
    values = jnp.concatenate(
        [jnp.where(at_fine, v, 0) for v in (jnp.ones_like(column), column // 128, column % 128)],
        axis=0,
    ).astype(jnp.bfloat16)
    found = lax.dot_general(
        in_coarse.astype(jnp.bfloat16),
        values,
        (((1,), (1,)), ((), ())),
        preferred_element_type=jnp.float32,
    )
    count, high, low = found[:, :fine], found[:, fine : 2 * fine], found[:, 2 * fine :]
    rank = jnp.where(count > 0.5, high * 128.0 + low, float(total)).astype(jnp.int32)
    return rank.reshape(rows_dev)


def split_in_kernel(value):
    head = value.astype(jnp.bfloat16)
    return head, (value - head.astype(jnp.float32)).astype(jnp.bfloat16)


LAST_FIRST = (((1,), (0,)), ((), ()))


def dot32(left, right, dims):
    return lax.dot_general(left, right, dims, preferred_element_type=jnp.float32)


def correction_kernel(place_ref, factor_ref, own_ref, other_ref, *refs, slim):
    out_refs, (head_ref, rest_ref) = refs[:-2], refs[-2:]

    @pl.when(pl.program_id(0) == 0)
    def _():
        for ref, core in ((own_ref, place_ref[1]), (other_ref, 1 - place_ref[1])):
            for block in range(ref.shape[0] // slim):
                rows = pl.ds(pl.multiple_of((2 * block + core) * slim, slim), slim)
                head_ref[rows, :], rest_ref[rows, :] = split_in_kernel(ref[pl.ds(block * slim, slim), :])

    block = factor_ref[...]
    product = dot32(block, head_ref[...], LAST_FIRST) + dot32(block, rest_ref[...], LAST_FIRST)
    for step, out_ref in enumerate(out_refs):

        @pl.when(pl.program_id(0) == step)
        def _(out_ref=out_ref):
            out_ref[...] = product


def factor_times(place, factor, own, other, slim):
    rows, cols = factor.shape
    width = own.shape[1]
    tile = rows // 4
    half = pl.BlockSpec((cols // 2, width), lambda i, place: (0, 0), pipeline_mode=pl.Buffered(1))
    return pl.pallas_call(
        functools.partial(correction_kernel, slim=slim),
        grid_spec=pltpu.PrefetchScalarGridSpec(
            num_scalar_prefetch=1,
            grid=(4,),
            in_specs=[
                pl.BlockSpec((tile, cols), lambda i, place: ((place[0] + i) % 4, 0)),
                half,
                half,
            ],
            out_specs=[pl.BlockSpec((tile, width), lambda i, place: (0, 0))] * 4,
            scratch_shapes=[pltpu.VMEM((cols, width), jnp.bfloat16)] * 2,
        ),
        out_shape=[jax.ShapeDtypeStruct((tile, width), jnp.float32)] * 4,
        cost_estimate=pl.CostEstimate(
            flops=4 * rows * cols * width,
            transcendentals=0,
            bytes_accessed=2 * rows * cols + 4 * cols * width + 4 * rows * width,
        ),
        name="factor_times",
    )(place, factor, own, other)


def outer_kernel(
    scale_ref, place_ref, cot_ref, probe_ref, w_own_ref, w_other_ref, d_own_ref, d_other_ref, rank_ref,
    out_ref, left_ref, *, slim,
):
    first_core = place_ref[1] == 0

    @pl.when(pl.program_id(0) == 0)
    def _():
        cot, probe = cot_ref[...], probe_ref[...]
        half = cot.shape[1] // 2
        turned = jnp.concatenate([cot[:, half:], cot[:, :half]], axis=1)
        cot = jnp.where(first_core, cot, turned)
        left_ref[...] = jnp.concatenate([cot, cot, probe, probe], axis=1)

    own, other = d_own_ref[...], d_other_ref[...]
    even, odd = jnp.where(first_core, own, other), jnp.where(first_core, other, own)
    blocks = []
    for at in range(0, own.shape[0], slim):
        blocks += [even[at : at + slim], odd[at : at + slim]]
    d_head, d_rest = split_in_kernel(jnp.concatenate(blocks, axis=0).T)
    own_head, own_rest = split_in_kernel(w_own_ref[...])
    other_head, other_rest = split_in_kernel(w_other_ref[...])
    right = jnp.concatenate([own_head, other_head, own_rest, other_rest, d_head, d_rest], axis=0)
    total = dot32(left_ref[...], right, LAST_FIRST) * (-1.0 / scale_ref[0])
    column = lax.broadcasted_iota(jnp.int32, total.shape, 1)
    limit = rank_ref[...] - (place_ref[0] + pl.program_id(0) * total.shape[1])
    out_ref[...] = jnp.where(column > limit, 0.0, total).astype(jnp.bfloat16)


def masked_outer(scale, place, cotangent, probes, w_own, w_other, d_own, d_other, pivot_rank, slim):
    rows, width = cotangent.shape
    cols = w_own.shape[1]
    tile = 256
    whole = pl.BlockSpec((rows, width), lambda j: (0, 0), pipeline_mode=pl.Buffered(1))
    w_spec = pl.BlockSpec((width // 2, tile), lambda j: (0, j))
    d_spec = pl.BlockSpec((tile // 2, width), lambda j: (j, 0))
    return pl.pallas_call(
        functools.partial(outer_kernel, slim=slim),
        grid=(cols // tile,),
        in_specs=[
            pl.BlockSpec(memory_space=pltpu.SMEM),
            pl.BlockSpec(memory_space=pltpu.SMEM),
            whole,
            whole,
            w_spec,
            w_spec,
            d_spec,
            d_spec,
            pl.BlockSpec((rows, 1), lambda j: (0, 0), pipeline_mode=pl.Buffered(1)),
        ],
        out_specs=pl.BlockSpec((rows, tile), lambda j: (0, j)),
        out_shape=jax.ShapeDtypeStruct((rows, cols), jnp.bfloat16),
        scratch_shapes=[pltpu.VMEM((rows, 4 * width), jnp.bfloat16)],
        cost_estimate=pl.CostEstimate(
            flops=8 * rows * cols * width,
            transcendentals=0,
            bytes_accessed=2 * rows * cols + 8 * cols * width + 4 * rows * width,
        ),
        name="masked_outer",
    )(scale, place, cotangent, probes, w_own, w_other, d_own, d_other, pivot_rank)


def body(factor, probes, cotangent, core_inverse, pivots, noise):
    rows_dev, block_cols = factor.shape
    width = probes.shape[1]
    n_rows = lax.axis_size("rows")
    n_rank = lax.axis_size("rank")
    slim = block_cols // n_rows
    scale = noise[0]
    core_tile = core_inverse.reshape(block_cols, n_rank * slim)
    contract = ((0,), (0,))

    core = place_of("core").astype(jnp.int32)
    dual = lax.dot_general(cotangent, factor, (contract, ((), ())), preferred_element_type=jnp.float32)
    coef = lax.dot_general(factor, probes, (contract, ((), ())), preferred_element_type=jnp.float32)

    dual = pair_sum(dual.reshape(2, width // 2, block_cols), "core", 0)
    coef = pair_sum(coef.reshape(4, 4, 2, slim, width), "core", 2)
    late_pivots = lax.optimization_barrier((pivots, coef))[0]
    pivot_rank = ranks_of_rows(late_pivots, rows_dev).reshape(rows_dev, 1)
    dual = halving(dual.reshape(4, width // 8, block_cols), "y", 0, 1, 3, (pivot_rank,))
    dual = dual + swapped(dual, "z", 2)
    dual = dual + swapped(dual, "z", 1)
    coef = halving(coef, "y", 1, 3, 1)
    coef = halving(coef, "z", 0, 1, 2)

    dual = gather(dual, "y", 0).reshape(width // 2, block_cols)
    dual_other = swapped(dual, "core", 1)
    coef = jnp.broadcast_to(coef[None], (n_rank, slim, width))
    coef = lax.all_to_all(coef, "rank", 0, 0)

    terms = zip(two_terms(dual), two_terms(dual_other))
    both = jnp.concatenate([term for pair in terms for term in pair], axis=0)
    duals = lax.dot_general(core_tile, both, (((0,), (1,)), ((), ())), preferred_element_type=jnp.float32)
    duals = duals[:, :width] + duals[:, width:]
    turned = jnp.concatenate([duals[:, width // 2 :], duals[:, : width // 2]], axis=1)
    duals = jnp.where(core == 0, duals, turned).reshape(n_rank, slim, width)
    coef = lax.optimization_barrier((coef, duals))[0].reshape(n_rank * slim, width)
    duals = jnp.sum(lax.all_to_all(duals, "rank", 0, 0), axis=0)
    head, rest = two_terms(coef)
    weights = lax.dot_general(head, core_tile, (((0,), (1,)), ((), ())), preferred_element_type=jnp.float32)
    weights = weights + lax.dot_general(
        rest, core_tile, (((0,), (1,)), ((), ())), preferred_element_type=jnp.float32
    )
    weights = pair_sum(weights.reshape(2, width // 2, block_cols), "core", 0)
    weights = halving(weights.reshape(4, width // 8, block_cols), "y", 0, 1, 3)

    duals = gather(duals, "z", 0)
    duals = gather(duals, "y", 1).reshape(block_cols // 2, width)
    duals_other = swapped(duals, "core", 1)
    me_x = place_of("x")
    pieces = factor_times(jnp.stack([me_x.astype(jnp.int32), core]), factor, duals, duals_other, slim)
    weights = weights + swapped(weights, "z", 2)
    arrived = lax.optimization_barrier((swapped(weights, "z", 1), *pieces))[0]
    weights = gather(weights + arrived, "y", 0).reshape(width // 2, block_cols)
    weights_other = swapped(weights, "core", 1)

    arrived = [shifted(piece, "x", step) for step, piece in enumerate(pieces) if step]
    correction = sum(arrived, pieces[0])
    correction = lax.optimization_barrier(correction + swapped(correction, "zhi", 1))
    blocks = cotangent.reshape(4, rows_dev // 4, width)
    probe_grad = jnp.zeros(blocks.shape, jnp.bfloat16)
    for step in range(4):
        piece = shifted(correction, "x", step) if step else correction
        at = lax.rem(me_x - step + 4, 4)
        piece = (pick(blocks, at, 0).astype(jnp.float32) - piece) / scale
        probe_grad = put(probe_grad, piece.astype(jnp.bfloat16), at, 0)
    probe_grad = probe_grad.reshape(rows_dev, width)

    first = (lax.axis_index("rank") * block_cols).astype(jnp.int32).reshape(1)
    grads = masked_outer(
        noise, jnp.concatenate([first, core.reshape(1)]), cotangent, probes,
        weights, weights_other, duals, duals_other, pivot_rank, slim,
    )
    return (probe_grad, grads)


def solution(mesh):
    placed = (
        P("rows", "rank"),
        P("rows", None),
        P("rows", None),
        P("rank", None, "rows"),
        P(),
        P(),
    )
    return jax.shard_map(
        body,
        mesh=mesh,
        in_specs=placed,
        out_specs=(P("rows", None), P("rows", "rank")),
        check_vma=False,
    )
```

```python
import functools

import jax
import jax.numpy as jnp
from jax import lax
from jax.experimental import pallas as pl
from jax.experimental.pallas import tpu as pltpu
from jax.sharding import PartitionSpec as P


PARTS = {
    "z": ("rows", 4, 8),
    "y": ("rows", 4, 2),
    "core": ("rows", 2, 1),
    "zhi": ("rank", 2, 4),
    "x": ("rank", 4, 1),
}


ARRIVALS = (3, 1, 2)


def place_of(part):
    axis, members, stride = PARTS[part]
    return lax.rem(lax.axis_index(axis) // stride, members)


def sent(value, part, move):
    axis, members, stride = PARTS[part]
    pairs = []
    for source in range(lax.axis_size(axis)):
        at = source // stride % members
        pairs.append((source, source + (move(at) - at) * stride))
    return lax.ppermute(value, axis, pairs)


def shifted(value, part, step):
    members = PARTS[part][1]
    return sent(value, part, lambda at: (at + step) % members)


def swapped(value, part, mask):
    return sent(value, part, lambda at: at ^ mask)


def pick(value, index, dim):
    return lax.dynamic_index_in_dim(value, index, dim, keepdims=False)


def put(whole, value, index, dim):
    return lax.dynamic_update_index_in_dim(whole, value, index, dim)


def gather(value, part, dim):
    members = PARTS[part][1]
    me = place_of(part)
    value = lax.optimization_barrier(value)
    shape = value.shape[:dim] + (members,) + value.shape[dim:]
    whole = put(jnp.zeros(shape, value.dtype), value, me, dim)
    for step in ARRIVALS:
        piece = shifted(value, part, step)
        whole = put(whole, piece, lax.rem(me - step + members, members), dim)
    return whole


def pair_sum(value, part, dim):
    me = place_of(part)
    return pick(value, me, dim) + swapped(pick(value, 1 - me, dim), part, 1)


def halving(value, part, dim, first, second, ahead=()):
    me = place_of(part)
    away = jnp.stack([pick(value, me ^ first, dim), pick(value, me ^ first ^ second, dim)])
    got = swapped(away, part, first)
    other = pick(value, me ^ second, dim) + got[1]
    other = lax.optimization_barrier((other, *ahead))[0]
    return pick(value, me, dim) + got[0] + swapped(other, part, second)


def two_terms(value):
    head = lax.reduce_precision(value, 8, 7)
    return head.astype(jnp.bfloat16), (value - head).astype(jnp.bfloat16)


def ranks_of_rows(pivots, rows_dev):
    total = pivots.shape[0]
    fine = 32
    local = pivots - lax.axis_index("rows") * rows_dev
    coarse = lax.broadcasted_iota(jnp.int32, (rows_dev // fine, total), 0)
    in_coarse = ((local // fine)[None, :] == coarse) & (local >= 0)[None, :]
    at_fine = lax.rem(local, fine)[None, :] == lax.broadcasted_iota(jnp.int32, (fine, total), 0)
    column = lax.broadcasted_iota(jnp.int32, (fine, total), 1)
    values = jnp.concatenate(
        [jnp.where(at_fine, v, 0) for v in (jnp.ones_like(column), column // 128, column % 128)],
        axis=0,
    ).astype(jnp.bfloat16)
    found = lax.dot_general(
        in_coarse.astype(jnp.bfloat16),
        values,
        (((1,), (1,)), ((), ())),
        preferred_element_type=jnp.float32,
    )
    count, high, low = found[:, :fine], found[:, fine : 2 * fine], found[:, 2 * fine :]
    rank = jnp.where(count > 0.5, high * 128.0 + low, float(total)).astype(jnp.int32)
    return rank.reshape(rows_dev)


def split_in_kernel(value):
    head = value.astype(jnp.bfloat16)
    return head, (value - head.astype(jnp.float32)).astype(jnp.bfloat16)


LAST_FIRST = (((1,), (0,)), ((), ()))


def dot32(left, right, dims):
    return lax.dot_general(left, right, dims, preferred_element_type=jnp.float32)


def correction_kernel(place_ref, factor_ref, own_ref, other_ref, *refs, slim):
    out_refs, (head_ref, rest_ref) = refs[:-2], refs[-2:]

    @pl.when(pl.program_id(0) == 0)
    def _():
        for ref, core in ((own_ref, place_ref[1]), (other_ref, 1 - place_ref[1])):
            for block in range(ref.shape[0] // slim):
                rows = pl.ds(pl.multiple_of((2 * block + core) * slim, slim), slim)
                head_ref[rows, :], rest_ref[rows, :] = split_in_kernel(ref[pl.ds(block * slim, slim), :])

    block = factor_ref[...]
    product = dot32(block, head_ref[...], LAST_FIRST) + dot32(block, rest_ref[...], LAST_FIRST)
    for step, out_ref in enumerate(out_refs):

        @pl.when(pl.program_id(0) == step)
        def _(out_ref=out_ref):
            out_ref[...] = product


def factor_times(place, factor, own, other, slim):
    rows, cols = factor.shape
    width = own.shape[1]
    tile = rows // 4
    half = pl.BlockSpec((cols // 2, width), lambda i, place: (0, 0), pipeline_mode=pl.Buffered(1))
    return pl.pallas_call(
        functools.partial(correction_kernel, slim=slim),
        grid_spec=pltpu.PrefetchScalarGridSpec(
            num_scalar_prefetch=1,
            grid=(4,),
            in_specs=[
                pl.BlockSpec((tile, cols), lambda i, place: ((place[0] + i) % 4, 0)),
                half,
                half,
            ],
            out_specs=[pl.BlockSpec((tile, width), lambda i, place: (0, 0))] * 4,
            scratch_shapes=[pltpu.VMEM((cols, width), jnp.bfloat16)] * 2,
        ),
        out_shape=[jax.ShapeDtypeStruct((tile, width), jnp.float32)] * 4,
        cost_estimate=pl.CostEstimate(
            flops=4 * rows * cols * width,
            transcendentals=0,
            bytes_accessed=2 * rows * cols + 4 * cols * width + 4 * rows * width,
        ),
        name="factor_times",
    )(place, factor, own, other)


def outer_kernel(
    scale_ref, place_ref, cot_ref, probe_ref, w_own_ref, w_other_ref, d_own_ref, d_other_ref, rank_ref,
    out_ref, left_ref, *, slim,
):
    first_core = place_ref[1] == 0

    @pl.when(pl.program_id(0) == 0)
    def _():
        cot, probe = cot_ref[...], probe_ref[...]
        half = cot.shape[1] // 2
        turned = jnp.concatenate([cot[:, half:], cot[:, :half]], axis=1)
        cot = jnp.where(first_core, cot, turned)
        left_ref[...] = jnp.concatenate([cot, cot, probe, probe], axis=1)

    own, other = d_own_ref[...], d_other_ref[...]
    even, odd = jnp.where(first_core, own, other), jnp.where(first_core, other, own)
    blocks = []
    for at in range(0, own.shape[0], slim):
        blocks += [even[at : at + slim], odd[at : at + slim]]
    d_head, d_rest = split_in_kernel(jnp.concatenate(blocks, axis=0).T)
    own_head, own_rest = split_in_kernel(w_own_ref[...])
    other_head, other_rest = split_in_kernel(w_other_ref[...])
    right = jnp.concatenate([own_head, other_head, own_rest, other_rest, d_head, d_rest], axis=0)
    total = dot32(left_ref[...], right, LAST_FIRST) * (-1.0 / scale_ref[0])
    column = lax.broadcasted_iota(jnp.int32, total.shape, 1)
    limit = rank_ref[...] - (place_ref[0] + pl.program_id(0) * total.shape[1])
    out_ref[...] = jnp.where(column > limit, 0.0, total).astype(jnp.bfloat16)


def masked_outer(scale, place, cotangent, probes, w_own, w_other, d_own, d_other, pivot_rank, slim):
    rows, width = cotangent.shape
    cols = w_own.shape[1]
    tile = 256
    whole = pl.BlockSpec((rows, width), lambda j: (0, 0), pipeline_mode=pl.Buffered(1))
    w_spec = pl.BlockSpec((width // 2, tile), lambda j: (0, j))
    d_spec = pl.BlockSpec((tile // 2, width), lambda j: (j, 0))
    return pl.pallas_call(
        functools.partial(outer_kernel, slim=slim),
        grid=(cols // tile,),
        in_specs=[
            pl.BlockSpec(memory_space=pltpu.SMEM),
            pl.BlockSpec(memory_space=pltpu.SMEM),
            whole,
            whole,
            w_spec,
            w_spec,
            d_spec,
            d_spec,
            pl.BlockSpec((rows, 1), lambda j: (0, 0), pipeline_mode=pl.Buffered(1)),
        ],
        out_specs=pl.BlockSpec((rows, tile), lambda j: (0, j)),
        out_shape=jax.ShapeDtypeStruct((rows, cols), jnp.bfloat16),
        scratch_shapes=[pltpu.VMEM((rows, 4 * width), jnp.bfloat16)],
        cost_estimate=pl.CostEstimate(
            flops=8 * rows * cols * width,
            transcendentals=0,
            bytes_accessed=2 * rows * cols + 8 * cols * width + 4 * rows * width,
        ),
        name="masked_outer",
    )(scale, place, cotangent, probes, w_own, w_other, d_own, d_other, pivot_rank)


def body(factor, probes, cotangent, core_inverse, pivots, noise):
    rows_dev, block_cols = factor.shape
    width = probes.shape[1]
    n_rows = lax.axis_size("rows")
    n_rank = lax.axis_size("rank")
    slim = block_cols // n_rows
    scale = noise[0]
    core_tile = core_inverse.reshape(block_cols, n_rank * slim)
    contract = ((0,), (0,))

    core = place_of("core").astype(jnp.int32)
    dual = lax.dot_general(cotangent, factor, (contract, ((), ())), preferred_element_type=jnp.float32)
    coef = lax.dot_general(factor, probes, (contract, ((), ())), preferred_element_type=jnp.float32)

    me_x = place_of("x")
    x_core = jnp.stack([me_x.astype(jnp.int32), core])
    first_core = jnp.stack([(lax.axis_index("rank") * block_cols).astype(jnp.int32), core])

    dual = pair_sum(dual.reshape(2, width // 2, block_cols), "core", 0)
    coef = pair_sum(coef.reshape(4, 4, 2, slim, width), "core", 2)
    late_pivots = lax.optimization_barrier((pivots, dual))[0]
    pivot_rank = ranks_of_rows(late_pivots, rows_dev).reshape(rows_dev, 1)
    dual = halving(dual.reshape(4, width // 8, block_cols), "y", 0, 1, 3, (pivot_rank, x_core, first_core))
    dual = dual + swapped(dual, "z", 2)
    dual = dual + swapped(dual, "z", 1)
    coef = halving(coef, "y", 1, 3, 1)
    coef = halving(coef, "z", 0, 1, 2)

    dual = gather(dual, "y", 0).reshape(width // 2, block_cols)
    dual_other = swapped(dual, "core", 1)
    coef = jnp.broadcast_to(coef[None], (n_rank, slim, width))
    coef = lax.all_to_all(coef, "rank", 0, 0)

    terms = zip(two_terms(dual), two_terms(dual_other))
    both = jnp.concatenate([term for pair in terms for term in pair], axis=0)
    duals = lax.dot_general(core_tile, both, (((0,), (1,)), ((), ())), preferred_element_type=jnp.float32)
    duals = duals[:, :width] + duals[:, width:]
    turned = jnp.concatenate([duals[:, width // 2 :], duals[:, : width // 2]], axis=1)
    duals = jnp.where(core == 0, duals, turned).reshape(n_rank, slim, width)
    coef = lax.optimization_barrier((coef, duals))[0].reshape(n_rank * slim, width)
    duals = jnp.sum(lax.all_to_all(duals, "rank", 0, 0), axis=0)
    head, rest = two_terms(coef)
    weights = lax.dot_general(head, core_tile, (((0,), (1,)), ((), ())), preferred_element_type=jnp.float32)
    weights = weights + lax.dot_general(
        rest, core_tile, (((0,), (1,)), ((), ())), preferred_element_type=jnp.float32
    )
    weights = pair_sum(weights.reshape(2, width // 2, block_cols), "core", 0)
    weights = halving(weights.reshape(4, width // 8, block_cols), "y", 0, 1, 3)

    duals = gather(duals, "z", 0)
    duals = gather(duals, "y", 1).reshape(block_cols // 2, width)
    duals_other = swapped(duals, "core", 1)
    pieces = factor_times(x_core, factor, duals, duals_other, slim)
    weights = weights + swapped(weights, "z", 2)
    arrived = lax.optimization_barrier((swapped(weights, "z", 1), *pieces))[0]
    weights = gather(weights + arrived, "y", 0).reshape(width // 2, block_cols)
    weights_other = swapped(weights, "core", 1)

    arrived = [shifted(piece, "x", step) for step, piece in enumerate(pieces) if step]
    correction = sum(arrived, pieces[0])
    correction = lax.optimization_barrier(correction + swapped(correction, "zhi", 1))
    blocks = cotangent.reshape(4, rows_dev // 4, width)
    probe_grad = jnp.zeros(blocks.shape, jnp.bfloat16)
    for step in (0, *ARRIVALS):
        piece = shifted(correction, "x", step) if step else correction
        at = lax.rem(me_x - step + 4, 4)
        piece = (pick(blocks, at, 0).astype(jnp.float32) - piece) / scale
        probe_grad = put(probe_grad, piece.astype(jnp.bfloat16), at, 0)
    probe_grad = probe_grad.reshape(rows_dev, width)

    grads = masked_outer(
        noise, first_core, cotangent, probes,
        weights, weights_other, duals, duals_other, pivot_rank, slim,
    )
    return (probe_grad, grads)


def solution(mesh):
    placed = (
        P("rows", "rank"),
        P("rows", None),
        P("rows", None),
        P("rank", None, "rows"),
        P(),
        P(),
    )
    return jax.shard_map(
        body,
        mesh=mesh,
        in_specs=placed,
        out_specs=(P("rows", None), P("rows", "rank")),
        check_vma=False,
    )
```

```python
import functools

import jax
import jax.numpy as jnp
from jax import lax
from jax.experimental import pallas as pl
from jax.experimental.pallas import tpu as pltpu
from jax.sharding import PartitionSpec as P


PARTS = {
    "z": ("rows", 4, 8),
    "y": ("rows", 4, 2),
    "core": ("rows", 2, 1),
    "zhi": ("rank", 2, 4),
    "x": ("rank", 4, 1),
}


ARRIVALS = (3, 1, 2)


def place_of(part):
    axis, members, stride = PARTS[part]
    return lax.rem(lax.axis_index(axis) // stride, members)


def sent(value, part, move):
    axis, members, stride = PARTS[part]
    pairs = []
    for source in range(lax.axis_size(axis)):
        at = source // stride % members
        pairs.append((source, source + (move(at) - at) * stride))
    return lax.ppermute(value, axis, pairs)


def shifted(value, part, step):
    members = PARTS[part][1]
    return sent(value, part, lambda at: (at + step) % members)


def swapped(value, part, mask):
    return sent(value, part, lambda at: at ^ mask)


def pick(value, index, dim):
    return lax.dynamic_index_in_dim(value, index, dim, keepdims=False)


def put(whole, value, index, dim):
    return lax.dynamic_update_index_in_dim(whole, value, index, dim)


def gather(value, part, dim):
    members = PARTS[part][1]
    me = place_of(part)
    value = lax.optimization_barrier(value)
    shape = value.shape[:dim] + (members,) + value.shape[dim:]
    whole = put(jnp.zeros(shape, value.dtype), value, me, dim)
    for step in ARRIVALS:
        piece = shifted(value, part, step)
        whole = put(whole, piece, lax.rem(me - step + members, members), dim)
    return whole


def pair_sum(value, part, dim):
    me = place_of(part)
    return pick(value, me, dim) + swapped(pick(value, 1 - me, dim), part, 1)


def halving(value, part, dim, first, second, ahead=()):
    me = place_of(part)
    away = jnp.stack([pick(value, me ^ first, dim), pick(value, me ^ first ^ second, dim)])
    got = swapped(away, part, first)
    other = pick(value, me ^ second, dim) + got[1]
    other = lax.optimization_barrier((other, *ahead))[0]
    return pick(value, me, dim) + got[0] + swapped(other, part, second)


def two_terms(value):
    head = lax.reduce_precision(value, 8, 7)
    return head.astype(jnp.bfloat16), (value - head).astype(jnp.bfloat16)


def ranks_of_rows(pivots, rows_dev):
    total = pivots.shape[0]
    fine = 32
    local = pivots - lax.axis_index("rows") * rows_dev
    coarse = lax.broadcasted_iota(jnp.int32, (rows_dev // fine, total), 0)
    in_coarse = ((local // fine)[None, :] == coarse) & (local >= 0)[None, :]
    at_fine = lax.rem(local, fine)[None, :] == lax.broadcasted_iota(jnp.int32, (fine, total), 0)
    column = lax.broadcasted_iota(jnp.int32, (fine, total), 1)
    values = jnp.concatenate(
        [jnp.where(at_fine, v, 0) for v in (jnp.ones_like(column), column // 128, column % 128)],
        axis=0,
    ).astype(jnp.bfloat16)
    found = lax.dot_general(
        in_coarse.astype(jnp.bfloat16),
        values,
        (((1,), (1,)), ((), ())),
        preferred_element_type=jnp.float32,
    )
    count, high, low = found[:, :fine], found[:, fine : 2 * fine], found[:, 2 * fine :]
    rank = jnp.where(count > 0.5, high * 128.0 + low, float(total)).astype(jnp.int32)
    return rank.reshape(rows_dev)


def split_in_kernel(value):
    head = value.astype(jnp.bfloat16)
    return head, (value - head.astype(jnp.float32)).astype(jnp.bfloat16)


LAST_FIRST = (((1,), (0,)), ((), ()))


def dot32(left, right, dims):
    return lax.dot_general(left, right, dims, preferred_element_type=jnp.float32)


def correction_kernel(place_ref, factor_ref, own_ref, other_ref, *refs, slim):
    out_refs, (head_ref, rest_ref) = refs[:-2], refs[-2:]

    @pl.when(pl.program_id(0) == 0)
    def _():
        for ref, core in ((own_ref, place_ref[1]), (other_ref, 1 - place_ref[1])):
            for block in range(ref.shape[0] // slim):
                rows = pl.ds(pl.multiple_of((2 * block + core) * slim, slim), slim)
                head_ref[rows, :], rest_ref[rows, :] = split_in_kernel(ref[pl.ds(block * slim, slim), :])

    block = factor_ref[...]
    product = dot32(block, head_ref[...], LAST_FIRST) + dot32(block, rest_ref[...], LAST_FIRST)
    for step, out_ref in enumerate(out_refs):

        @pl.when(pl.program_id(0) == step)
        def _(out_ref=out_ref):
            out_ref[...] = product


def factor_times(place, factor, own, other, slim):
    rows, cols = factor.shape
    width = own.shape[1]
    tile = rows // 4
    half = pl.BlockSpec((cols // 2, width), lambda i, place: (0, 0), pipeline_mode=pl.Buffered(1))
    return pl.pallas_call(
        functools.partial(correction_kernel, slim=slim),
        grid_spec=pltpu.PrefetchScalarGridSpec(
            num_scalar_prefetch=1,
            grid=(4,),
            in_specs=[
                pl.BlockSpec((tile, cols), lambda i, place: ((place[0] + i) % 4, 0)),
                half,
                half,
            ],
            out_specs=[pl.BlockSpec((tile, width), lambda i, place: (0, 0))] * 4,
            scratch_shapes=[pltpu.VMEM((cols, width), jnp.bfloat16)] * 2,
        ),
        out_shape=[jax.ShapeDtypeStruct((tile, width), jnp.float32)] * 4,
        cost_estimate=pl.CostEstimate(
            flops=4 * rows * cols * width,
            transcendentals=0,
            bytes_accessed=2 * rows * cols + 4 * cols * width + 4 * rows * width,
        ),
        name="factor_times",
    )(place, factor, own, other)


def outer_kernel(
    scale_ref, place_ref, cot_ref, probe_ref, w_own_ref, w_other_ref, d_own_ref, d_other_ref, rank_ref,
    out_ref, left_ref, *, slim,
):
    first_core = place_ref[1] == 0

    @pl.when(pl.program_id(0) == 0)
    def _():
        cot, probe = cot_ref[...], probe_ref[...]
        half = cot.shape[1] // 2
        turned = jnp.concatenate([cot[:, half:], cot[:, :half]], axis=1)
        cot = jnp.where(first_core, cot, turned)
        left_ref[...] = jnp.concatenate([cot, cot, probe, probe], axis=1)

    own, other = d_own_ref[...], d_other_ref[...]
    even, odd = jnp.where(first_core, own, other), jnp.where(first_core, other, own)
    blocks = []
    for at in range(0, own.shape[0], slim):
        blocks += [even[at : at + slim], odd[at : at + slim]]
    d_head, d_rest = split_in_kernel(jnp.concatenate(blocks, axis=0).T)
    own_head, own_rest = split_in_kernel(w_own_ref[...])
    other_head, other_rest = split_in_kernel(w_other_ref[...])
    right = jnp.concatenate([own_head, other_head, own_rest, other_rest, d_head, d_rest], axis=0)
    total = dot32(left_ref[...], right, LAST_FIRST) * (-1.0 / scale_ref[0])
    column = lax.broadcasted_iota(jnp.int32, total.shape, 1)
    limit = rank_ref[...] - (place_ref[0] + pl.program_id(0) * total.shape[1])
    out_ref[...] = jnp.where(column > limit, 0.0, total).astype(jnp.bfloat16)


def masked_outer(scale, place, cotangent, probes, w_own, w_other, d_own, d_other, pivot_rank, slim):
    rows, width = cotangent.shape
    cols = w_own.shape[1]
    tile = 256
    whole = pl.BlockSpec((rows, width), lambda j: (0, 0), pipeline_mode=pl.Buffered(1))
    w_spec = pl.BlockSpec((width // 2, tile), lambda j: (0, j))
    d_spec = pl.BlockSpec((tile // 2, width), lambda j: (j, 0))
    return pl.pallas_call(
        functools.partial(outer_kernel, slim=slim),
        grid=(cols // tile,),
        in_specs=[
            pl.BlockSpec(memory_space=pltpu.SMEM),
            pl.BlockSpec(memory_space=pltpu.SMEM),
            whole,
            whole,
            w_spec,
            w_spec,
            d_spec,
            d_spec,
            pl.BlockSpec((rows, 1), lambda j: (0, 0), pipeline_mode=pl.Buffered(1)),
        ],
        out_specs=pl.BlockSpec((rows, tile), lambda j: (0, j)),
        out_shape=jax.ShapeDtypeStruct((rows, cols), jnp.bfloat16),
        scratch_shapes=[pltpu.VMEM((rows, 4 * width), jnp.bfloat16)],
        cost_estimate=pl.CostEstimate(
            flops=8 * rows * cols * width,
            transcendentals=0,
            bytes_accessed=2 * rows * cols + 8 * cols * width + 4 * rows * width,
        ),
        name="masked_outer",
    )(scale, place, cotangent, probes, w_own, w_other, d_own, d_other, pivot_rank)


def body(factor, probes, cotangent, core_inverse, pivots, noise):
    rows_dev, block_cols = factor.shape
    width = probes.shape[1]
    n_rows = lax.axis_size("rows")
    n_rank = lax.axis_size("rank")
    slim = block_cols // n_rows
    scale = noise[0]
    core_tile = core_inverse.reshape(block_cols, n_rank * slim)
    contract = ((0,), (0,))

    core = place_of("core").astype(jnp.int32)
    dual = lax.dot_general(cotangent, factor, (contract, ((), ())), preferred_element_type=jnp.float32)
    coef = lax.dot_general(factor, probes, (contract, ((), ())), preferred_element_type=jnp.float32)

    me_x = place_of("x")
    x_core = jnp.stack([me_x.astype(jnp.int32), core])
    first_core = jnp.stack([(lax.axis_index("rank") * block_cols).astype(jnp.int32), core])

    dual = pair_sum(dual.reshape(2, width // 2, block_cols), "core", 0)
    coef = pair_sum(coef.reshape(4, 4, 2, slim, width), "core", 2)
    late_pivots = lax.optimization_barrier((pivots, dual))[0]
    pivot_rank = ranks_of_rows(late_pivots, rows_dev).reshape(rows_dev, 1)
    dual = halving(dual.reshape(4, width // 8, block_cols), "y", 0, 1, 3, (pivot_rank, x_core, first_core))
    dual = dual + swapped(dual, "z", 2)
    dual = dual + swapped(dual, "z", 1)
    coef = halving(coef, "y", 1, 3, 1)
    coef = halving(coef, "z", 0, 1, 2)

    dual = gather(dual, "y", 0).reshape(width // 2, block_cols)
    dual_other = swapped(dual, "core", 1)
    coef = jnp.broadcast_to(coef[None], (n_rank, slim, width))
    coef = lax.all_to_all(coef, "rank", 0, 0)

    terms = zip(two_terms(dual), two_terms(dual_other))
    both = jnp.concatenate([term for pair in terms for term in pair], axis=0)
    duals = lax.dot_general(core_tile, both, (((0,), (1,)), ((), ())), preferred_element_type=jnp.float32)
    duals = duals[:, :width] + duals[:, width:]
    turned = jnp.concatenate([duals[:, width // 2 :], duals[:, : width // 2]], axis=1)
    duals = jnp.where(core == 0, duals, turned).reshape(n_rank, slim, width)
    coef = lax.optimization_barrier((coef, duals))[0].reshape(n_rank * slim, width)
    duals = jnp.sum(lax.all_to_all(duals, "rank", 0, 0), axis=0)
    head, rest = two_terms(coef)
    weights = lax.dot_general(head, core_tile, (((0,), (1,)), ((), ())), preferred_element_type=jnp.float32)
    weights = weights + lax.dot_general(
        rest, core_tile, (((0,), (1,)), ((), ())), preferred_element_type=jnp.float32
    )
    weights = pair_sum(weights.reshape(2, width // 2, block_cols), "core", 0)
    weights = halving(weights.reshape(4, width // 8, block_cols), "y", 0, 1, 3)

    duals = gather(duals, "z", 0)
    duals = gather(duals, "y", 1).reshape(block_cols // 2, width)
    duals_other = swapped(duals, "core", 1)
    pieces = factor_times(x_core, factor, duals, duals_other, slim)
    arrived = lax.optimization_barrier((swapped(weights, "z", 2), *pieces))[0]
    weights = weights + arrived
    weights = weights + swapped(weights, "z", 1)
    weights = gather(weights, "y", 0).reshape(width // 2, block_cols)
    weights_other = swapped(weights, "core", 1)

    arrived = [shifted(piece, "x", step) for step, piece in enumerate(pieces) if step]
    correction = sum(arrived, pieces[0])
    correction = lax.optimization_barrier(correction + swapped(correction, "zhi", 1))
    blocks = cotangent.reshape(4, rows_dev // 4, width)
    probe_grad = jnp.zeros(blocks.shape, jnp.bfloat16)
    for step in (0, *ARRIVALS):
        piece = shifted(correction, "x", step) if step else correction
        at = lax.rem(me_x - step + 4, 4)
        piece = (pick(blocks, at, 0).astype(jnp.float32) - piece) / scale
        probe_grad = put(probe_grad, piece.astype(jnp.bfloat16), at, 0)
    probe_grad = probe_grad.reshape(rows_dev, width)

    grads = masked_outer(
        noise, first_core, cotangent, probes,
        weights, weights_other, duals, duals_other, pivot_rank, slim,
    )
    return (probe_grad, grads)


def solution(mesh):
    placed = (
        P("rows", "rank"),
        P("rows", None),
        P("rows", None),
        P("rank", None, "rows"),
        P(),
        P(),
    )
    return jax.shard_map(
        body,
        mesh=mesh,
        in_specs=placed,
        out_specs=(P("rows", None), P("rows", "rank")),
        check_vma=False,
    )
```
